32 devices in a mesh: lat: 8 (over z, x), lon: 4 (over y, core).
Axes of the slice: x: 2, y: 2, z: 4, core: 2. Of those that a mesh axis runs over, the one named last changes fastest.
Arguments:
- adjoint_in: float32 [128, 128, 1024], P(None, 'lat', 'lon'), may hold values from -6 to 6
- obs_adjoint: float32 [65536, 128], P(('lat', 'lon')), may hold values from -6 to 6
- obs_owner: int32 [65536, 1], P(('lat', 'lon')), may hold values from 0 to 31; in each aligned block of 2048 rows (0 to 2047, 2048 to 4095, ...) at most 128 rows name the same one
- obs_column: int32 [65536], P(('lat', 'lon')), may hold values from 0 to 4095
- winds: float32 [3, 2, 32, 128, 1024], P(None, None, None, 'lat', 'lon'), may hold values from -0.3 to 0.3
- diffusion: float32 [128], replicated, may hold values from 0.03 to 0.12
Outputs:
- adjoint_out: float32 [128, 128, 1024], P(None, 'lat', 'lon')
The draws below stay inside these ranges and needn't reach their ends.
Inputs may be any that keep to these rules, and one draw needn't show every extreme that they name: `obs_owner`: in each aligned block of 2048 observations (one shard's), no owner is named more than 128 times, a bound that some block reaches.
All inputs are finite; a program needn't handle non-finite values.
Results may differ from the reference program's by a relative error of at most 0.00002.
Values sent between devices are 32-bit elements; how exact they have to be, the bound alone decides.
A program may use at most 64 MiB of HBM per device.

```python
import math
import jax
import jax.numpy as jnp
import numpy as np

LEVELS = 32
STEPS = 3
CLAT = 16
CLON = 256
OBS_DEV = 2048
CHAN = 128
CAP = 128
NLAT = 128
NLON = 1024
TOTAL_OBS = 65536
N_LON = 4
DEVICES = 32


def plant(result, stream_key, smallest, largest):
    shape = result.shape
    spot = [jax.random.randint(jax.random.fold_in(stream_key, axis), (), 0, shape[axis]) for axis in range(len(shape))]
    result = result.at[tuple(spot)].set(smallest)
    longest = shape.index(max(shape))
    spot[longest] = (spot[longest] + 1) % shape[longest]
    return result.at[tuple(spot)].set(largest)


def block_scale(own_key, shape, cuts, smallest, largest):
    gain, own = 1.0, jax.random.fold_in(own_key, 6)
    for axis_at, shards_of in cuts:
        draws = jnp.exp(jax.random.uniform(jax.random.fold_in(own, axis_at), (shards_of,), jnp.float32, smallest / len(cuts), largest / len(cuts)))
        gain = gain * jnp.repeat(draws, shape[axis_at] // shards_of).reshape([-1 if axis == axis_at else 1 for axis in range(len(shape))])
    return gain


def deal_out(key, own, number, rows, number_of, top, bound, skew):
    order = jax.random.permutation(key, number_of)
    packed, ordinary = load_shares(number_of, rows * top, bound, skew, True), load_shares(number_of, rows * top, bound, skew, False)
    places = jnp.arange(number_of)

    def named(tallies, rotation):
        used = int((tallies > 0).sum())
        fixed = max(1, used // 4)
        shifted = fixed + (places - fixed + rotation * (used - fixed)) % max(1, number_of - fixed)
        return jnp.zeros((number_of,), jnp.int32).at[order[jnp.where(places < fixed, places, shifted)]].set(jnp.asarray(tallies, jnp.int32))

    tallies = jnp.where(number % 4 == 0, named(packed, number // 4), named(ordinary, number - number // 4 - 1))
    mixed = jax.random.permutation(jax.random.fold_in(own, 3), number_of)
    source_of, receiver = mixed[0:number_of // 2 * 2:2], mixed[1:number_of // 2 * 2:2]
    room = jnp.minimum(tallies[source_of] - 1, bound - tallies[receiver]) // 2
    room = jnp.where((source_of == order[0]) | (receiver == order[0]) | (tallies[receiver] == 0), 0, jnp.maximum(room, 0))
    shifted = jax.random.randint(jax.random.fold_in(own, 4), (number_of // 2,), 0, 1 << 20) % (room + 1)
    tallies = tallies.at[source_of].add(-shifted).at[receiver].add(shifted)
    labels = jnp.searchsorted(jnp.cumsum(tallies), jnp.arange(rows * top), side="right").astype(jnp.int32)
    table = labels.reshape(top, rows).T
    table = table[jax.random.permutation(jax.random.fold_in(own, 1), rows)]
    rotation = jax.random.randint(jax.random.fold_in(own, 2), (rows, 1), 0, top)
    return jnp.take_along_axis(table, (jnp.arange(top)[None, :] + rotation) % top, axis=1)


def load_shares(amount, total, most, skew, full):
    weights = [(1 << 20) // math.isqrt(standing ** skew) + 1 for standing in range(1, amount + 1)]
    largest = most if full else min(most, max(-(-total // amount), total * weights[0] // sum(weights)))
    least = 1 if total - largest >= amount - 1 else 0
    holding, surplus = [largest] + [least] * (amount - 1), total - largest - least * (amount - 1)
    while surplus > 0:
        free = [i for i in range(1, amount) if holding[i] < largest] or [i for i in range(1, amount) if holding[i] < most]
        mass, budget = sum([weights[i] for i in free]), surplus
        for i in free:
            extra = min(most - holding[i], max(1, budget * weights[i] // mass), surplus)
            holding[i] = holding[i] + extra
            surplus = surplus - extra
    return np.array(holding)


def scatter_about(key, shape, scale, bound, split=(), held_as=jnp.bfloat16):
    values = jax.random.normal(key, shape, jnp.float32) * scale
    if len(split) > 0:
        values = block_scale(key, shape, split, -0.22, 0.18) * values
    return jnp.clip(values, min=-bound, max=bound).astype(held_as)


def setup_inputs(seed: int = 0) -> dict:
    seeds = jax.random.split(jax.random.key(seed), 7)
    adjoint_in = scatter_about(seeds[0], (CHAN, NLAT, NLON), 1.0, 6.0, ((1, 8), (2, 4)), jnp.float32)
    obs_adjoint = scatter_about(seeds[1], (TOTAL_OBS, CHAN), 1.0, 6.0, ((0, 32),), jnp.float32)
    obs_owner_keys = jax.random.split(jax.random.fold_in(seeds[2], 1), TOTAL_OBS // OBS_DEV)
    obs_owner_turns = jax.random.permutation(jax.random.fold_in(seeds[2], 3), TOTAL_OBS // OBS_DEV)
    obs_owner = jax.vmap(lambda own, number: deal_out(jax.random.fold_in(seeds[2], 2), own, number, OBS_DEV, DEVICES, 1, CAP, 1))(obs_owner_keys, obs_owner_turns).reshape((TOTAL_OBS, 1))
    obs_column = plant(jax.random.randint(seeds[3], (TOTAL_OBS,), 0, CLAT * CLON), jax.random.fold_in(seeds[3], 1), 0, (CLAT * CLON) - 1).astype(jnp.int32)
    winds = jnp.clip(jax.random.uniform(seeds[4], (STEPS, 2, LEVELS, NLAT, NLON), jnp.float32, -0.3, 0.3) * block_scale(seeds[4], (STEPS, 2, LEVELS, NLAT, NLON), ((3, 8), (4, 4)), -0.4, 0.0), -0.3, 0.3)
    diffusion = jnp.clip(jnp.exp(jax.random.uniform(seeds[5], (CHAN,), jnp.float32, math.log(0.03), math.log(0.12))), 0.03, 0.12)
    return {"adjoint_in": adjoint_in, "obs_adjoint": obs_adjoint, "obs_owner": obs_owner, "obs_column": obs_column, "winds": winds, "diffusion": diffusion}


def advance(grid, east, north, diffusion):
    lev = east.shape[0]
    g = grid.reshape(-1, lev, grid.shape[1], grid.shape[2])
    k = diffusion.reshape(-1, lev)[:, :, None, None]
    core = g[:, :, 1:-1, 1:-1]
    u_east = east[None, :, 1:-1, 1:-1]
    u_west = east[None, :, 1:-1, :-2]
    v_north = north[None, :, 1:-1, 1:-1]
    v_south = north[None, :, :-2, 1:-1]
    out = core + (g[:, :, 1:-1, 2:] - core) * (0.5 * u_east + k)
    out = out + (core - g[:, :, 1:-1, :-2]) * (0.5 * u_west - k)
    out = out + (g[:, :, 2:, 1:-1] - core) * (0.5 * v_north + k)
    out = out + (core - g[:, :, :-2, 1:-1]) * (0.5 * v_south - k)
    return out.reshape(-1, out.shape[2], out.shape[3])


def extend(field):
    wrapped = jnp.pad(field, ((0, 0), (0, 0), (1, 1)), mode="wrap")
    return jnp.pad(wrapped, ((0, 0), (1, 1), (0, 0)))


def reference(adjoint_in, obs_adjoint, obs_owner, obs_column, winds, diffusion):
    owner = obs_owner[:, 0]
    glob_row = (owner // N_LON) * CLAT + obs_column // CLON
    glob_col = (owner % N_LON) * CLON + obs_column % CLON
    flat = (glob_row * NLON + glob_col).astype(jnp.int32)
    forcing = jnp.zeros((NLAT * NLON, CHAN), jnp.float32).at[flat].add(obs_adjoint)
    state = adjoint_in + forcing.T.reshape(CHAN, NLAT, NLON)
    for step in range(STEPS):
        s = STEPS - 1 - step
        state = advance(extend(state), extend(winds[s, 0]), extend(winds[s, 1]), diffusion)
    return state
```

```python
import functools

import jax
import jax.numpy as jnp
from jax import lax
from jax.experimental import pallas as pl
from jax.experimental.pallas import tpu as pltpu
from jax.sharding import PartitionSpec as P

STEPS = 3
LANES = 128
META = 8
JOIN = 4
TWIST = 13
UNROLL = 5
F32 = jnp.float32
BF16 = jnp.bfloat16
NT = (((1,), (1,)), ((), ()))


def halves(x):
    high = x.astype(BF16)
    return high, (x - high.astype(F32)).astype(BF16)


def kernel(
    n_lat, n_lon,
    obs_ref, owner_ref, column_ref, diffusion_ref, adj_ref, winds_ref, out_ref,
    obs, k_ref, half, wind_west, wind_south, pieces, rank_ref, send_v, recv_v, lhs,
    state_a, state_b, winds, row_halo, col_send, col_halo, wind_row, wind_send, wind_col,
    obs_sem, adj_sem, wind_sem, self_sem, sv_sem, rv_sem, hs_sem, hr_sem, ws_sem, wr_sem, out_sem,
):
    lat = lax.axis_index("lat")
    lon = lax.axis_index("lon")
    n = n_lat * n_lon
    me = lat * n_lon + lon
    rows, chan = obs.shape
    lat_rows, _, lon_cols = state_a.shape
    lev = winds.shape[3]
    fields = chan // lev
    lane = lax.broadcasted_iota(jnp.int32, (1, LANES), 1)

    def device(d):
        return (lax.div(d, n_lon), lax.rem(d, n_lon))

    def remote(src, dst, send, recv, to):
        return pltpu.make_async_remote_copy(
            src_ref=src, dst_ref=dst, send_sem=send, recv_sem=recv,
            device_id=to, device_id_type=pl.DeviceIdType.MESH,
        )

    width = 256
    blocks = rows // width

    def load_obs(b):
        span = pl.ds(b * width, width)
        return pltpu.make_async_copy(obs_ref.at[span], obs.at[span], obs_sem.at[b])

    for b in range(blocks):
        load_obs(b).start()

    barrier = pltpu.get_barrier_semaphore()

    def greet(k, _):
        pl.semaphore_signal(
            barrier, inc=1, device_id=device(lax.rem(me + k, n)),
            device_id_type=pl.DeviceIdType.MESH,
        )
        return 0

    lax.fori_loop(1, n, greet, 0)

    def load_row(l):
        return pltpu.make_async_copy(adj_ref.at[:, l, :], state_a.at[l], adj_sem.at[l])

    def load_wind(s, w, l):
        return pltpu.make_async_copy(
            winds_ref.at[s, w, :, l, :], winds.at[s, w, l], wind_sem.at[s, w, l]
        )

    def each_row(act):
        lax.fori_loop(0, lat_rows, lambda l, _: act(l) or 0, 0)

    def each_wind(act):
        for s in range(STEPS):
            for w in range(2):
                lax.fori_loop(0, lat_rows, lambda l, _: act(s, w, l) or 0, 0)

    each_wind(lambda s, w, l: load_wind(s, w, l).start())
    each_row(lambda l: load_row(l).start())

    below = lax.broadcasted_iota(jnp.int32, (width, width), 0)
    along = lax.broadcasted_iota(jnp.int32, (width, width), 1)
    before = jnp.where(below < along, 1.0, 0.0).astype(BF16)
    carry = jnp.zeros((n, 1), F32)
    owners = lax.broadcasted_iota(jnp.int32, (n, width), 0)
    sub = lax.broadcasted_iota(jnp.int32, (16, width), 0)
    for b in range(blocks):
        span = slice(b * width, (b + 1) * width)
        owner = owner_ref[:, span]
        hot = jnp.where(owners == owner, 1.0, 0.0)
        rank = jnp.dot(hot.astype(BF16), before, preferred_element_type=F32) + carry
        rank_ref[:, span] = jnp.sum(hot * rank, axis=0, keepdims=True).astype(jnp.int32) + owner * LANES
        carry = carry + jnp.sum(hot, axis=1, keepdims=True)
        column = column_ref[:, span]
        if lon_cols & (lon_cols - 1):
            row = jnp.floor((column.astype(F32) + 0.5) * (1.0 / lon_cols)).astype(jnp.int32)
        else:
            row = column >> (lon_cols.bit_length() - 1)
        turned = column - row * lon_cols + row + 1
        turned = jnp.where(turned >= lon_cols, turned - lon_cols, turned)
        pieces[2 * chan:, span] = jnp.where(
            sub == 0, row, jnp.where(sub == 1, turned, 0)
        ).astype(F32).astype(BF16)
        load_obs(b).wait()
        high, low = halves(obs[span, :].T)
        pieces[:chan, span] = high
        pieces[chan:2 * chan, span] = low
    pl.semaphore_wait(barrier, n - 1)

    each_wind(lambda s, w, l: load_wind(s, w, l).wait())
    for s in range(STEPS):
        col = jnp.zeros((lev, LANES), F32)
        for l in range(lat_rows):
            tile = winds[s, 0, l, :, lon_cols - LANES:]
            col = jnp.where(lane == l, tile[:, LANES - 1:], col)
        wind_send[s] = col

    @pl.when(lat == 0)
    def _():
        wind_row[...] = jnp.zeros_like(wind_row)
        for t in range(STEPS):
            row_halo[t, 0] = jnp.zeros((chan, lon_cols), F32)

    @pl.when(lat == n_lat - 1)
    def _():
        for t in range(STEPS):
            row_halo[t, 1] = jnp.zeros((chan, lon_cols), F32)

    east = (lat, lax.rem(lon + 1, n_lon))
    west = (lat, lax.rem(lon + n_lon - 1, n_lon))
    north = (lax.rem(lat + 1, n_lat), lon)
    south = (lax.rem(lat + n_lat - 1, n_lat), lon)

    send_wind_col = remote(wind_send, wind_col, ws_sem.at[0], wr_sem.at[0], east)
    send_wind_col.start()

    def wind_row_copy(s):
        return remote(
            winds.at[s, 1, lat_rows - 1], wind_row.at[s],
            ws_sem.at[1 + s], wr_sem.at[1 + s], north,
        )

    @pl.when(lat < n_lat - 1)
    def _():
        for s in range(STEPS):
            wind_row_copy(s).start()

    def message(ref, d, f):
        if f == 0:
            return ref.at[d, pl.ds(0, META + lev)]
        return ref.at[d, pl.ds(META + f * lev, lev)]

    def value_copy(d, f):
        return remote(
            message(send_v, d, f), message(recv_v, me, f),
            sv_sem.at[f, d], rv_sem.at[f, me], device(d),
        )

    def arrival(src, f):
        return remote(
            message(send_v, src, f), message(recv_v, src, f),
            sv_sem.at[f, src], rv_sem.at[f, src], device(src),
        )

    def own_copy():
        return pltpu.make_async_copy(send_v.at[me], recv_v.at[me], self_sem)

    def target(g):
        return lax.rem(me + TWIST * (g + 1), n)

    def source(g):
        return lax.rem(me + (n - TWIST % n) * (g + 1), n)

    def pack(p, _):
        hots = []
        for q in range(2):
            d = target(2 * p + q)
            slots = lax.broadcasted_iota(jnp.int32, (LANES, rows), 0) + d * LANES
            hots.append(jnp.where(slots == rank_ref[...], 1.0, 0.0).astype(BF16))
        both = lax.dot_general(
            pieces[...], jnp.concatenate(hots, axis=0), NT, preferred_element_type=F32
        )
        for q in range(2):
            d = target(2 * p + q)
            at = slice(q * LANES, (q + 1) * LANES)
            send_v[d, META:] = both[:chan, at] + both[chan:2 * chan, at]
            send_v[d, :META] = both[2 * chan:2 * chan + META, at]

            @pl.when(d != me)
            def _():
                value_copy(d, 0).start()

            @pl.when(d == me)
            def _():
                own_copy().start()

        return 0

    lax.fori_loop(0, n // 2, pack, 0)

    def send_field(f):
        def start(g, _):
            value_copy(target(g), f).start()
            return 0

        lax.fori_loop(0, n - 1, start, 0)

    if fields > 1:
        send_field(1)

    k_tile = jnp.broadcast_to(diffusion_ref[...], (LANES, chan)).T
    for j in range(lon_cols // LANES):
        k_ref[:, j * LANES:(j + 1) * LANES] = k_tile
    each_row(lambda l: load_row(l).wait())

    def skew(l, _):
        state_a[l] = pltpu.roll(state_a[l], l + 1, 1)
        return 0

    lax.fori_loop(0, lat_rows, skew, 0)

    def prepare():
        send_wind_col.wait()

        @pl.when(lat < n_lat - 1)
        def _():
            for s in range(STEPS):
                wind_row_copy(s).wait_send()

        @pl.when(lat > 0)
        def _():
            for s in range(STEPS):
                wind_row_copy(s).wait_recv()

        first = lax.broadcasted_iota(jnp.int32, (lev, lon_cols), 1) == 0
        for s in range(STEPS):
            def halve(l, _):
                u = winds[s, 0, l]
                edge = pltpu.roll(wind_col[s], lax.rem(LANES - l, LANES), 1)
                edge = jnp.concatenate([edge] * (lon_cols // LANES), axis=1)
                half[s, 0, l] = 0.5 * pltpu.roll(u, l + 1, 1)
                half[s, 1, l] = 0.5 * pltpu.roll(winds[s, 1, l], l + 1, 1)
                wind_west[s, l] = 0.5 * pltpu.roll(jnp.where(first, edge, pltpu.roll(u, 1, 1)), l + 1, 1)
                south_wind = winds[s, 1, jnp.maximum(l - 1, 0)]
                south_wind = jnp.where(l == 0, wind_row[s], south_wind)
                wind_south[s, l] = 0.5 * pltpu.roll(south_wind, l + 1, 1)
                return 0

            lax.fori_loop(0, lat_rows, halve, 0)

    def unpack_field(f):
        part = slice(f * lev, (f + 1) * lev)

        def unpack(p, _):
            for j in range(2 * JOIN):
                src = source(p * 2 * JOIN + j)

                @pl.when(src != me)
                def _():
                    arrival(src, f).wait_recv()

                if f == 0:
                    @pl.when(src == me)
                    def _():
                        own_copy().wait()

            for c in range(2):
                highs, lows, places = [], [], []
                for j in range(JOIN):
                    src = source((p * 2 + c) * JOIN + j)
                    high, low = halves(recv_v[src, META + f * lev:META + (f + 1) * lev])
                    highs.append(high)
                    lows.append(low)
                    places.append(recv_v[src, :META])
                values = jnp.concatenate(highs + lows, axis=1)
                cell = jnp.concatenate(places, axis=1)
                lons = lax.broadcasted_iota(jnp.int32, (lon_cols, cell.shape[1]), 0)
                hot = jnp.where(lons == cell[1:2].astype(jnp.int32), 1.0, 0.0).astype(BF16)
                hot = jnp.concatenate([hot, hot], axis=1)
                row = cell[0:1].astype(jnp.int32)
                row = jnp.concatenate([row, row], axis=1)
                for l in range(lat_rows):
                    mask = jnp.where(row == l, 1.0, 0.0).astype(BF16)
                    lhs[c, l * lev:(l + 1) * lev, :] = values * mask
                add = lax.dot_general(lhs[c], hot, NT, preferred_element_type=F32)
                for l in range(lat_rows):
                    state_a[l, part] += add[l * lev:(l + 1) * lev]
            return 0

        lax.fori_loop(0, n // (2 * JOIN), unpack, 0)

    def halo_copies(t, f):
        now = state_b if t % 2 else state_a
        part = pl.ds(f * lev, lev)
        pairs = (
            (now.at[lat_rows - 1, part], row_halo.at[t, 0, part], north),
            (now.at[0, part], row_halo.at[t, 1, part], south),
            (col_send.at[t, 0, part], col_halo.at[t, 0, part], east),
            (col_send.at[t, 1, part], col_halo.at[t, 1, part], west),
        )
        return [
            remote(src, dst, hs_sem.at[t, f, i], hr_sem.at[t, f, i], to)
            for i, (src, dst, to) in enumerate(pairs)
        ]

    def send_halos(t, f, low, high):
        part = slice(f * lev, (f + 1) * lev)
        to_north, to_south, to_east, to_west = halo_copies(t, f)

        @pl.when(lat < n_lat - 1)
        def _():
            to_north.start()

        @pl.when(lat > 0)
        def _():
            to_south.start()

        col_send[t, 0, part, :] = pltpu.roll(high, 1, 1)
        col_send[t, 1, part, :] = pltpu.roll(low, LANES - 1, 1)
        to_east.start()
        to_west.start()

    def wait_halos(t, f):
        to_north, to_south, to_east, to_west = halo_copies(t, f)

        @pl.when(lat > 0)
        def _():
            to_north.wait_recv()
            to_south.wait_send()

        @pl.when(lat < n_lat - 1)
        def _():
            to_south.wait_recv()
            to_north.wait_send()

        to_east.wait()
        to_west.wait()

    blank = jnp.zeros((lev, LANES), F32)

    def first_halos(f):
        part = slice(f * lev, (f + 1) * lev)
        low = high = blank
        for l in range(lat_rows):
            tile = state_a[l, part, :LANES]
            low = jnp.where(lane == l + 1, tile, low)
            high = jnp.where(lane == l, tile, high)
        send_halos(0, f, low, high)

    def head_of(x, at, ends):
        return jnp.concatenate([jnp.where(lane == at, ends, x[:, :LANES]), x[:, LANES:]], axis=1)

    def store_row(l, f):
        part = pl.ds(f * lev, lev)
        return pltpu.make_async_copy(
            state_b.at[l, part], out_ref.at[part, l, :], out_sem.at[f, l]
        )

    def advance(t, f):
        s = STEPS - 1 - t
        now, later = (state_a, state_b) if t % 2 == 0 else (state_b, state_a)
        part = slice(f * lev, (f + 1) * lev)
        wait_halos(t, f)
        k = k_ref[part, :]
        ends_west = col_halo[t, 0, part, :]
        ends_east = col_halo[t, 1, part, :]

        def row(l, below, core, e, above, low, high):
            w = pltpu.roll(core, 1, 1)
            new = core + (head_of(e, l, ends_east) - core) * (half[s, 0, l] + k)
            new = new + (core - head_of(w, l + 1, ends_west)) * (wind_west[s, l] - k)
            new = new + (above - core) * (half[s, 1, l] + k)
            new = new + (core - below) * (wind_south[s, l] - k)
            if t == STEPS - 1:
                later[l, part, :] = pltpu.roll(new, lon_cols - 1 - l, 1)
            else:
                later[l, part, :] = new
                low = jnp.where(lane == l + 1, new[:, :LANES], low)
                high = jnp.where(lane == l, new[:, :LANES], high)
            return w, low, high

        def inner(l, state):
            below, core, e, low, high = state
            following = now[l + 1, part, :]
            above = pltpu.roll(following, lon_cols - 1, 1)
            w, low, high = row(l, below, core, e, above, low, high)
            return w, following, above, low, high

        below = pltpu.roll(row_halo[t, 0, part, :], lon_cols - (lat_rows - 1), 1)
        core = now[0, part, :]
        e = pltpu.roll(core, lon_cols - 1, 1)
        below, core, e, low, high = lax.fori_loop(
            0, lat_rows - 1, inner, (below, core, e, blank, blank), unroll=UNROLL
        )
        above = pltpu.roll(row_halo[t, 1, part, :], lat_rows - 1, 1)
        _, low, high = row(lat_rows - 1, below, core, e, above, low, high)
        if t < STEPS - 1:
            send_halos(t + 1, f, low, high)
        else:
            each_row(lambda l: store_row(l, f).start())

    prepare()
    for slot in range(fields + STEPS):
        if slot < fields:
            unpack_field(slot)
            first_halos(slot)
            if slot + 2 < fields:
                send_field(slot + 2)
        for t in range(STEPS):
            f = slot - 1 - t
            if 0 <= f < fields:
                advance(t, f)

    for f in range(fields):
        def drain(g, _):
            value_copy(target(g), f).wait_send()
            return 0

        lax.fori_loop(0, n - 1, drain, 0)
        each_row(lambda l: store_row(l, f).wait())


def local(adjoint_in, obs_adjoint, obs_owner, obs_column, winds, diffusion):
    chan, lat_rows, lon_cols = adjoint_in.shape
    steps, _, lev = winds.shape[:3]
    n_lat = lax.axis_size("lat")
    n_lon = lax.axis_size("lon")
    n = n_lat * n_lon
    rows = obs_adjoint.shape[0]
    fields = chan // lev
    owner = obs_owner.reshape(1, rows)
    column = obs_column.reshape(1, rows)
    k = diffusion.reshape(1, chan)
    vmem = pl.BlockSpec(memory_space=pltpu.VMEM)
    hbm = pl.BlockSpec(memory_space=pl.ANY)
    dma = pltpu.SemaphoreType.DMA
    return pl.pallas_call(
        functools.partial(kernel, n_lat, n_lon),
        out_shape=jax.ShapeDtypeStruct((chan, lat_rows, lon_cols), F32),
        in_specs=[hbm, vmem, vmem, vmem, hbm, hbm],
        out_specs=hbm,
        scratch_shapes=[
            pltpu.VMEM((rows, chan), F32),
            pltpu.VMEM((chan, lon_cols), F32),
            pltpu.VMEM((steps, 2, lat_rows, lev, lon_cols), F32),
            pltpu.VMEM((steps, lat_rows, lev, lon_cols), F32),
            pltpu.VMEM((steps, lat_rows, lev, lon_cols), F32),
            pltpu.VMEM((2 * chan + 16, rows), BF16),
            pltpu.VMEM((1, rows), jnp.int32),
            pltpu.VMEM((n, META + chan, LANES), F32),
            pltpu.VMEM((n, META + chan, LANES), F32),
            pltpu.VMEM((2, lat_rows * lev, 2 * JOIN * LANES), BF16),
            pltpu.VMEM((lat_rows, chan, lon_cols), F32),
            pltpu.VMEM((lat_rows, chan, lon_cols), F32),
            pltpu.VMEM((steps, 2, lat_rows, lev, lon_cols), F32),
            pltpu.VMEM((steps, 2, chan, lon_cols), F32),
            pltpu.VMEM((steps, 2, chan, LANES), F32),
            pltpu.VMEM((steps, 2, chan, LANES), F32),
            pltpu.VMEM((steps, lev, lon_cols), F32),
            pltpu.VMEM((steps, lev, LANES), F32),
            pltpu.VMEM((steps, lev, LANES), F32),
            dma((rows // 256,)), dma((lat_rows,)), dma((steps, 2, lat_rows)), dma,
            dma((fields, n)), dma((fields, n)),
            dma((steps, fields, 4)), dma((steps, fields, 4)), dma((1 + steps,)), dma((1 + steps,)),
            dma((fields, lat_rows)),
        ],
        compiler_params=pltpu.CompilerParams(
            collective_id=0, has_side_effects=True, vmem_limit_bytes=60 * 1024 * 1024
        ),
    )(obs_adjoint, owner, column, k, adjoint_in, winds)


def solution(mesh):
    placed = (
        P(None, "lat", "lon"),
        P(("lat", "lon"), None),
        P(("lat", "lon"), None),
        P(("lat", "lon")),
        P(None, None, None, "lat", "lon"),
        P(),
    )
    return jax.shard_map(
        local, mesh=mesh, in_specs=placed, out_specs=P(None, "lat", "lon"), check_vma=False
    )
```

```python
import functools

import jax
import jax.numpy as jnp
from jax import lax
from jax.experimental import pallas as pl
from jax.experimental.pallas import tpu as pltpu
from jax.sharding import PartitionSpec as P

STEPS = 3
LANES = 128
SPLIT = 0
JOIN = 4
TWIST = 13
UNROLL = 7
F32 = jnp.float32
BF16 = jnp.bfloat16
NT = (((1,), (1,)), ((), ()))


def plan(chan, lev):
    fields = chan // lev
    cut = lev // 2 if lev % 16 == 0 else lev
    sizes = [lev if f < fields - SPLIT else cut for f in range(fields)]
    return [
        (f * lev + at, at, size)
        for f, size in enumerate(sizes) for at in range(0, lev, size)
    ]


def halves(x):
    high = x.astype(BF16)
    return high, (x - high.astype(F32)).astype(BF16)


def kernel(
    n_lat, n_lon,
    obs_ref, owner_ref, column_ref, diffusion_ref, adj_ref, winds_ref, out_ref,
    obs, k_ref, half, wind_west, wind_south, pieces, rank_ref, send_v, recv_v, send_c, recv_c, lhs,
    state_a, state_b, winds, row_halo, col_send, col_halo, wind_row, wind_send, wind_col,
    obs_sem, adj_sem, wind_sem, self_sem, sv_sem, rv_sem, sc_sem, rc_sem, hs_sem, hr_sem, ws_sem, wr_sem, out_sem,
):
    lat = lax.axis_index("lat")
    lon = lax.axis_index("lon")
    n = n_lat * n_lon
    me = lat * n_lon + lon
    rows, chan = obs.shape
    lat_rows, _, lon_cols = state_a.shape
    lev = winds.shape[3]
    chunks = plan(chan, lev)
    lane = lax.broadcasted_iota(jnp.int32, (1, LANES), 1)

    def device(d):
        return (lax.div(d, n_lon), lax.rem(d, n_lon))

    def remote(src, dst, send, recv, to):
        return pltpu.make_async_remote_copy(
            src_ref=src, dst_ref=dst, send_sem=send, recv_sem=recv,
            device_id=to, device_id_type=pl.DeviceIdType.MESH,
        )

    width = 256
    blocks = rows // width

    def load_obs(b):
        span = pl.ds(b * width, width)
        return pltpu.make_async_copy(obs_ref.at[span], obs.at[span], obs_sem.at[b])

    for b in range(blocks):
        load_obs(b).start()

    barrier = pltpu.get_barrier_semaphore()

    def greet(k, _):
        pl.semaphore_signal(
            barrier, inc=1, device_id=device(lax.rem(me + k, n)),
            device_id_type=pl.DeviceIdType.MESH,
        )
        return 0

    lax.fori_loop(1, n, greet, 0)

    def load_row(l):
        return pltpu.make_async_copy(adj_ref.at[:, l, :], state_a.at[l], adj_sem.at[l])

    def load_wind(s, w, l):
        return pltpu.make_async_copy(
            winds_ref.at[s, w, :, l, :], winds.at[s, w, l], wind_sem.at[s, w, l]
        )

    def each_row(act):
        lax.fori_loop(0, lat_rows, lambda l, _: act(l) or 0, 0)

    def each_wind(act):
        for s in range(STEPS):
            for w in range(2):
                lax.fori_loop(0, lat_rows, lambda l, _: act(s, w, l) or 0, 0)

    each_wind(lambda s, w, l: load_wind(s, w, l).start())
    each_row(lambda l: load_row(l).start())

    below = lax.broadcasted_iota(jnp.int32, (width, width), 0)
    along = lax.broadcasted_iota(jnp.int32, (width, width), 1)
    before = jnp.where(below < along, 1.0, 0.0).astype(BF16)
    carry = jnp.zeros((n, 1), F32)
    owners = lax.broadcasted_iota(jnp.int32, (n, width), 0)
    sub = lax.broadcasted_iota(jnp.int32, (16, width), 0)
    for b in range(blocks):
        span = slice(b * width, (b + 1) * width)
        owner = owner_ref[:, span]
        hot = jnp.where(owners == owner, 1.0, 0.0)
        rank = jnp.dot(hot.astype(BF16), before, preferred_element_type=F32) + carry
        rank_ref[:, span] = jnp.sum(hot * rank, axis=0, keepdims=True).astype(jnp.int32) + owner * LANES
        carry = carry + jnp.sum(hot, axis=1, keepdims=True)
        column = column_ref[:, span]
        if lon_cols & (lon_cols - 1):
            row = jnp.floor((column.astype(F32) + 0.5) * (1.0 / lon_cols)).astype(jnp.int32)
        else:
            row = column >> (lon_cols.bit_length() - 1)
        turned = column - row * lon_cols + row + 1
        turned = jnp.where(turned >= lon_cols, turned - lon_cols, turned)
        pieces[2 * chan:, span] = jnp.where(
            sub == 0, row, jnp.where(sub == 1, turned, 0)
        ).astype(F32).astype(BF16)
        load_obs(b).wait()
        high, low = halves(obs[span, :].T)
        pieces[:chan, span] = high
        pieces[chan:2 * chan, span] = low
    pl.semaphore_wait(barrier, n - 1)

    def message(ref, d, f):
        base, _, size = chunks[f]
        return ref.at[d, pl.ds(base, size)]

    def value_copy(d, f):
        return remote(
            message(send_v, d, f), message(recv_v, me, f),
            sv_sem.at[f, d], rv_sem.at[f, me], device(d),
        )

    def arrival(src, f):
        return remote(
            message(send_v, src, f), message(recv_v, src, f),
            sv_sem.at[f, src], rv_sem.at[f, src], device(src),
        )

    def cell_copy(d):
        return remote(send_c.at[d], recv_c.at[me], sc_sem.at[d], rc_sem.at[me], device(d))

    def cell_arrival(src):
        return remote(send_c.at[src], recv_c.at[src], sc_sem.at[src], rc_sem.at[src], device(src))

    def own_copies():
        return (
            pltpu.make_async_copy(send_v.at[me], recv_v.at[me], self_sem.at[0]),
            pltpu.make_async_copy(send_c.at[me], recv_c.at[me], self_sem.at[1]),
        )

    def target(g):
        return lax.rem(me + TWIST * (g + 1), n)

    def source(g):
        return lax.rem(me + (n - TWIST % n) * (g + 1), n)

    def pack(p, _):
        hots = []
        for q in range(2):
            d = target(2 * p + q)
            slots = lax.broadcasted_iota(jnp.int32, (LANES, rows), 0) + d * LANES
            hots.append(jnp.where(slots == rank_ref[...], 1.0, 0.0).astype(BF16))
        both = lax.dot_general(
            pieces[...], jnp.concatenate(hots, axis=0), NT, preferred_element_type=F32
        )
        for q in range(2):
            d = target(2 * p + q)
            at = slice(q * LANES, (q + 1) * LANES)
            send_v[d] = both[:chan, at] + both[chan:2 * chan, at]
            send_c[d] = both[2 * chan:2 * chan + 1, at] * lon_cols + both[2 * chan + 1:2 * chan + 2, at]

            @pl.when(d != me)
            def _():
                cell_copy(d).start()
                value_copy(d, 0).start()

            @pl.when(d == me)
            def _():
                for copy in own_copies():
                    copy.start()

        return 0

    lax.fori_loop(0, 1, pack, 0)
    each_wind(lambda s, w, l: load_wind(s, w, l).wait())
    for s in range(STEPS):
        col = jnp.zeros((lev, LANES), F32)
        for l in range(lat_rows):
            tile = winds[s, 0, l, :, lon_cols - LANES:]
            col = jnp.where(lane == l, tile[:, LANES - 1:], col)
        wind_send[s] = col

    @pl.when(lat == 0)
    def _():
        wind_row[...] = jnp.zeros_like(wind_row)
        for t in range(STEPS):
            row_halo[t, 0] = jnp.zeros((chan, lon_cols), F32)

    @pl.when(lat == n_lat - 1)
    def _():
        for t in range(STEPS):
            row_halo[t, 1] = jnp.zeros((chan, lon_cols), F32)

    east = (lat, lax.rem(lon + 1, n_lon))
    west = (lat, lax.rem(lon + n_lon - 1, n_lon))
    north = (lax.rem(lat + 1, n_lat), lon)
    south = (lax.rem(lat + n_lat - 1, n_lat), lon)

    send_wind_col = remote(wind_send, wind_col, ws_sem.at[0], wr_sem.at[0], east)
    send_wind_col.start()

    def wind_row_copy(s):
        return remote(
            winds.at[s, 1, lat_rows - 1], wind_row.at[s],
            ws_sem.at[1 + s], wr_sem.at[1 + s], north,
        )

    @pl.when(lat < n_lat - 1)
    def _():
        for s in range(STEPS):
            wind_row_copy(s).start()
    lax.fori_loop(1, n // 2, pack, 0)

    def send_field(f):
        def start(g, _):
            value_copy(target(g), f).start()
            return 0

        lax.fori_loop(0, n - 1, start, 0)

    if len(chunks) > 1:
        send_field(1)

    k_tile = jnp.broadcast_to(diffusion_ref[...], (LANES, chan)).T
    for j in range(lon_cols // LANES):
        k_ref[:, j * LANES:(j + 1) * LANES] = k_tile
    each_row(lambda l: load_row(l).wait())

    def skew(l, _):
        state_a[l] = pltpu.roll(state_a[l], l + 1, 1)
        return 0

    lax.fori_loop(0, lat_rows, skew, 0)

    def prepare():
        send_wind_col.wait()

        @pl.when(lat < n_lat - 1)
        def _():
            for s in range(STEPS):
                wind_row_copy(s).wait_send()

        @pl.when(lat > 0)
        def _():
            for s in range(STEPS):
                wind_row_copy(s).wait_recv()

        first = lax.broadcasted_iota(jnp.int32, (lev, lon_cols), 1) == 0
        for s in range(STEPS):
            def halve(l, _):
                u = winds[s, 0, l]
                edge = pltpu.roll(wind_col[s], lax.rem(LANES - l, LANES), 1)
                edge = jnp.concatenate([edge] * (lon_cols // LANES), axis=1)
                half[s, 0, l] = 0.5 * pltpu.roll(u, l + 1, 1)
                half[s, 1, l] = 0.5 * pltpu.roll(winds[s, 1, l], l + 1, 1)
                wind_west[s, l] = 0.5 * pltpu.roll(jnp.where(first, edge, pltpu.roll(u, 1, 1)), l + 1, 1)
                south_wind = winds[s, 1, jnp.maximum(l - 1, 0)]
                south_wind = jnp.where(l == 0, wind_row[s], south_wind)
                wind_south[s, l] = 0.5 * pltpu.roll(south_wind, l + 1, 1)
                return 0

            lax.fori_loop(0, lat_rows, halve, 0)

    def unpack_field(f):
        base, _, size = chunks[f]
        part = slice(base, base + size)

        def unpack(p, _):
            for j in range(2 * JOIN):
                src = source(p * 2 * JOIN + j)

                @pl.when(src != me)
                def _():
                    arrival(src, f).wait_recv()
                    if f == 0:
                        cell_arrival(src).wait_recv()

                if f == 0:
                    @pl.when(src == me)
                    def _():
                        for copy in own_copies():
                            copy.wait()

            for c in range(2):
                highs, lows, places = [], [], []
                for j in range(JOIN):
                    src = source((p * 2 + c) * JOIN + j)
                    high, low = halves(recv_v[src, base:base + size])
                    highs.append(high)
                    lows.append(low)
                    places.append(recv_c[src])
                values = jnp.concatenate(highs + lows, axis=1)
                cell = jnp.concatenate(places, axis=1)
                lons = lax.broadcasted_iota(jnp.int32, (lon_cols, cell.shape[1]), 0)
                row = jnp.floor((cell + 0.5) * (1.0 / lon_cols))
                turned = (cell - row * lon_cols).astype(jnp.int32)
                hot = jnp.where(lons == turned, 1.0, 0.0).astype(BF16)
                hot = jnp.concatenate([hot, hot], axis=1)
                row = row.astype(jnp.int32)
                row = jnp.concatenate([row, row], axis=1)
                for l in range(lat_rows):
                    mask = jnp.where(row == l, 1.0, 0.0).astype(BF16)
                    lhs[c, l * size:(l + 1) * size, :] = values * mask
                add = lax.dot_general(lhs[c, :lat_rows * size], hot, NT, preferred_element_type=F32)
                for l in range(lat_rows):
                    state_a[l, part] += add[l * size:(l + 1) * size]
            return 0

        lax.fori_loop(0, n // (2 * JOIN), unpack, 0)

    def halo_copies(t, f):
        now = state_b if t % 2 else state_a
        base, _, size = chunks[f]
        part = pl.ds(base, size)
        pairs = (
            (now.at[lat_rows - 1, part], row_halo.at[t, 0, part], north),
            (now.at[0, part], row_halo.at[t, 1, part], south),
            (col_send.at[t, 0, part], col_halo.at[t, 0, part], east),
            (col_send.at[t, 1, part], col_halo.at[t, 1, part], west),
        )
        return [
            remote(src, dst, hs_sem.at[t, f, i], hr_sem.at[t, f, i], to)
            for i, (src, dst, to) in enumerate(pairs)
        ]

    def send_rows(t, f):
        to_north, to_south, _, _ = halo_copies(t, f)

        @pl.when(lat < n_lat - 1)
        def _():
            to_north.start()

        @pl.when(lat > 0)
        def _():
            to_south.start()

    def send_columns(t, f, low, high):
        base, _, size = chunks[f]
        part = slice(base, base + size)
        _, _, to_east, to_west = halo_copies(t, f)
        col_send[t, 0, part, :] = pltpu.roll(high, 1, 1)
        col_send[t, 1, part, :] = pltpu.roll(low, LANES - 1, 1)
        to_east.start()
        to_west.start()

    def wait_halos(t, f):
        to_north, to_south, to_east, to_west = halo_copies(t, f)
        to_east.wait()
        to_west.wait()

        @pl.when(lat > 0)
        def _():
            to_north.wait_recv()
            to_south.wait_send()

        @pl.when(lat < n_lat - 1)
        def _():
            to_south.wait_recv()
            to_north.wait_send()

    def first_halos(f):
        base, _, size = chunks[f]
        part = slice(base, base + size)
        send_rows(0, f)
        low = high = jnp.zeros((size, LANES), F32)
        for l in range(lat_rows):
            tile = state_a[l, part, :LANES]
            low = jnp.where(lane == l + 1, tile, low)
            high = jnp.where(lane == l, tile, high)
        send_columns(0, f, low, high)

    def head_of(x, at, ends):
        return jnp.concatenate([jnp.where(lane == at, ends, x[:, :LANES]), x[:, LANES:]], axis=1)

    def store_row(l, f):
        base, _, size = chunks[f]
        part = pl.ds(base, size)
        return pltpu.make_async_copy(
            state_b.at[l, part], out_ref.at[part, l, :], out_sem.at[f, l]
        )

    def advance(t, f):
        s = STEPS - 1 - t
        now, later = (state_a, state_b) if t % 2 == 0 else (state_b, state_a)
        base, level, size = chunks[f]
        part = slice(base, base + size)
        levs = slice(level, level + size)
        final = t == STEPS - 1
        last = lat_rows - 1
        wait_halos(t, f)
        k = k_ref[part, :]
        ends_west = col_halo[t, 0, part, :]
        ends_east = col_halo[t, 1, part, :]

        def left(x):
            return pltpu.roll(x, lon_cols - 1, 1)

        def row(l, below, core, e, above, low, high):
            w = pltpu.roll(core, 1, 1)
            new = core + (head_of(e, l, ends_east) - core) * (half[s, 0, l, levs] + k)
            new = new + (core - head_of(w, l + 1, ends_west)) * (wind_west[s, l, levs] - k)
            new = new + (above - core) * (half[s, 1, l, levs] + k)
            new = new + (core - below) * (wind_south[s, l, levs] - k)
            if final:
                later[l, part, :] = pltpu.roll(new, lon_cols - 1 - l, 1)
            else:
                later[l, part, :] = new
                low = jnp.where(lane == l + 1, new[:, :LANES], low)
                high = jnp.where(lane == l, new[:, :LANES], high)
            return w, low, high

        def inner(l, state):
            below, core, e, low, high = state
            following = now[l + 1, part, :]
            above = left(following)
            w, low, high = row(l, below, core, e, above, low, high)
            return w, following, above, low, high

        low = high = jnp.zeros((size, LANES), F32)
        below = pltpu.roll(row_halo[t, 0, part, :], lon_cols - last, 1)
        core = now[0, part, :]
        following = now[1, part, :]
        e = left(following)
        w, low, high = row(0, below, core, left(core), e, low, high)
        below = pltpu.roll(now[last - 1, part, :], 1, 1)
        core = now[last, part, :]
        above = pltpu.roll(row_halo[t, 1, part, :], last, 1)
        _, low, high = row(last, below, core, left(core), above, low, high)
        if not final:
            send_rows(t + 1, f)
        _, _, _, low, high = lax.fori_loop(
            1, last, inner, (w, following, e, low, high), unroll=UNROLL
        )
        if final:
            each_row(lambda l: store_row(l, f).start())
        else:
            send_columns(t + 1, f, low, high)

    prepare()
    for slot in range(len(chunks) + STEPS):
        if slot < len(chunks):
            if slot + 2 < len(chunks):
                send_field(slot + 2)
            unpack_field(slot)
            first_halos(slot)
        for t in range(STEPS):
            f = slot - 1 - t
            if 0 <= f < len(chunks):
                advance(t, f)

    for f in range(len(chunks)):
        def drain(g, _):
            value_copy(target(g), f).wait_send()
            if f == 0:
                cell_copy(target(g)).wait_send()
            return 0

        lax.fori_loop(0, n - 1, drain, 0)
        each_row(lambda l: store_row(l, f).wait())


def local(adjoint_in, obs_adjoint, obs_owner, obs_column, winds, diffusion):
    chan, lat_rows, lon_cols = adjoint_in.shape
    steps, _, lev = winds.shape[:3]
    n_lat = lax.axis_size("lat")
    n_lon = lax.axis_size("lon")
    n = n_lat * n_lon
    rows = obs_adjoint.shape[0]
    parts = len(plan(chan, lev))
    owner = obs_owner.reshape(1, rows)
    column = obs_column.reshape(1, rows)
    k = diffusion.reshape(1, chan)
    vmem = pl.BlockSpec(memory_space=pltpu.VMEM)
    hbm = pl.BlockSpec(memory_space=pltpu.HBM)
    dma = pltpu.SemaphoreType.DMA
    return pl.pallas_call(
        functools.partial(kernel, n_lat, n_lon),
        out_shape=pltpu.VMEM((chan, lat_rows, lon_cols), F32),
        in_specs=[hbm, vmem, vmem, vmem, hbm, hbm],
        out_specs=vmem,
        scratch_shapes=[
            pltpu.VMEM((rows, chan), F32),
            pltpu.VMEM((chan, lon_cols), F32),
            pltpu.VMEM((steps, 2, lat_rows, lev, lon_cols), F32),
            pltpu.VMEM((steps, lat_rows, lev, lon_cols), F32),
            pltpu.VMEM((steps, lat_rows, lev, lon_cols), F32),
            pltpu.VMEM((2 * chan + 16, rows), BF16),
            pltpu.VMEM((1, rows), jnp.int32),
            pltpu.VMEM((n, chan, LANES), F32),
            pltpu.VMEM((n, chan, LANES), F32),
            pltpu.VMEM((n, 1, LANES), F32),
            pltpu.VMEM((n, 1, LANES), F32),
            pltpu.VMEM((2, lat_rows * lev, 2 * JOIN * LANES), BF16),
            pltpu.VMEM((lat_rows, chan, lon_cols), F32),
            pltpu.VMEM((lat_rows, chan, lon_cols), F32),
            pltpu.VMEM((steps, 2, lat_rows, lev, lon_cols), F32),
            pltpu.VMEM((steps, 2, chan, lon_cols), F32),
            pltpu.VMEM((steps, 2, chan, LANES), F32),
            pltpu.VMEM((steps, 2, chan, LANES), F32),
            pltpu.VMEM((steps, lev, lon_cols), F32),
            pltpu.VMEM((steps, lev, LANES), F32),
            pltpu.VMEM((steps, lev, LANES), F32),
            dma((rows // 256,)), dma((lat_rows,)), dma((steps, 2, lat_rows)), dma((2,)),
            dma((parts, n)), dma((parts, n)), dma((n,)), dma((n,)),
            dma((steps, parts, 4)), dma((steps, parts, 4)), dma((1 + steps,)), dma((1 + steps,)),
            dma((parts, lat_rows)),
        ],
        compiler_params=pltpu.CompilerParams(
            collective_id=0, has_side_effects=True, vmem_limit_bytes=60 * 1024 * 1024
        ),
    )(obs_adjoint, owner, column, k, adjoint_in, winds)


def solution(mesh):
    placed = (
        P(None, "lat", "lon"),
        P(("lat", "lon"), None),
        P(("lat", "lon"), None),
        P(("lat", "lon")),
        P(None, None, None, "lat", "lon"),
        P(),
    )
    return jax.shard_map(
        local, mesh=mesh, in_specs=placed, out_specs=P(None, "lat", "lon"), check_vma=False
    )
```
